32 devices in a mesh: wide: 8 (over y, x, core), narrow: 4 (over z).
Axes of the slice: x: 2, y: 2, z: 4, core: 2. Of those that a mesh axis runs over, the one named last changes fastest.
Arguments:
- tokens: bfloat16 [128, 512, 768], P(('wide', 'narrow')), may hold values from -6 to 6
- lengths: int32 [128], P(('wide', 'narrow')), may hold values from 128 to 512, as said below
- query_lengths: int32 [128], P(('wide', 'narrow')), may hold values from 2 to 64
- language_ids: int32 [128], P(('wide', 'narrow')), may hold values from 0 to 99
- position_table: bfloat16 [512, 768], P('wide', 'narrow'), may hold values from -3 to 3
- segment_table: bfloat16 [2, 768], replicated, may hold values from -3 to 3
- language_table: bfloat16 [100, 768], replicated, may hold values from -3 to 3
- query_weight: bfloat16 [768, 768], P('wide', 'narrow'), may hold values from -0.21875 to 0.21875
- key_weight: bfloat16 [768, 768], P('wide', 'narrow'), may hold values from -0.21875 to 0.21875
- value_weight: bfloat16 [768, 768], P('wide', 'narrow'), may hold values from -0.21875 to 0.21875
- output_weight: bfloat16 [768, 768], P('wide', 'narrow'), may hold values from -0.875 to 0.875
- query_bias: bfloat16 [768], replicated, may hold values from -2 to 2
- value_bias: bfloat16 [768], replicated, may hold values from -2 to 2
- output_bias: bfloat16 [768], replicated, may hold values from -2 to 2
- first_gain: bfloat16 [768], replicated, may hold values from 0.5 to 1.5
- first_shift: bfloat16 [768], replicated, may hold values from -2 to 2
- up_weight: bfloat16 [768, 3072], P('wide', 'narrow'), may hold values from -0.21875 to 0.21875
- up_bias: bfloat16 [3072], replicated, may hold values from -2 to 2
- down_weight: bfloat16 [3072, 768], P('wide', 'narrow'), may hold values from -0.109375 to 0.109375
- down_bias: bfloat16 [768], replicated, may hold values from -2 to 2
- second_gain: bfloat16 [768], replicated, may hold values from 0.5 to 1.5
- second_shift: bfloat16 [768], replicated, may hold values from -2 to 2
- cotangent: bfloat16 [128, 512, 768], P(('wide', 'narrow')), may hold values from -6 to 6
Outputs:
- layer_out: bfloat16 [128, 512, 768], P(('wide', 'narrow'))
- token_grad: bfloat16 [128, 512, 768], P(('wide', 'narrow'))
- position_grad: float32 [512, 768], P('wide', 'narrow')
- segment_grad: float32 [2, 768], replicated
- language_grad: float32 [100, 768], replicated
- query_weight_grad: float32 [768, 768], P('wide', 'narrow')
- key_weight_grad: float32 [768, 768], P('wide', 'narrow')
- value_weight_grad: float32 [768, 768], P('wide', 'narrow')
- output_weight_grad: float32 [768, 768], P('wide', 'narrow')
- query_bias_grad: float32 [768], replicated
- value_bias_grad: float32 [768], replicated
- output_bias_grad: float32 [768], replicated
- first_gain_grad: float32 [768], replicated
- first_shift_grad: float32 [768], replicated
- up_weight_grad: float32 [768, 3072], P('wide', 'narrow')
- up_bias_grad: float32 [3072], replicated
- down_weight_grad: float32 [3072, 768], P('wide', 'narrow')
- down_bias_grad: float32 [768], replicated
- second_gain_grad: float32 [768], replicated
- second_shift_grad: float32 [768], replicated
The draws below stay inside these ranges and needn't reach their ends.
Inputs may be any that keep to these rules, and one draw needn't show every extreme that they name: Each pair has lengths live tokens, the rest are padding; some pair fills all 512 positions. `query_lengths`: A pair's queries lie within its live tokens.
All inputs are finite; a program needn't handle non-finite values.
Results may differ from the reference program's by a relative error of at most 0.015.
The reference program's roundings to bfloat16 on the way count: a program that leaves them out, or rounds other values in their place, can miss the bound.
Values may be sent and summed in bfloat16 or wider, within the bound.
No kernel may reach another device: no remote copies, remote signals or barrier semaphores. Data moves between devices by JAX's collectives and lax.ppermute only.
A program may use at most 256 MiB of HBM per device.

```python
import math
import jax
import jax.numpy as jnp
from jax import lax

D = 768
H = 12
HD = 64
FF = 3072
SEQ = 512
NLANG = 100
SEQS = 128


def draw_lengths(key, part):
    lengths_drawn = jax.random.randint(key, (SEQS,), SEQ // 4, SEQ + 1)
    chosen = jax.random.randint(jax.random.fold_in(key, 7), (), 0, SEQS)
    return jnp.where(jnp.arange(SEQS) == chosen, SEQ, lengths_drawn).astype(jnp.int32)


def plant(result, stream_key, low, top_value):
    longest = result.shape.index(max(result.shape))
    spots = []
    for shift in (0, 1):
        where = [jax.random.randint(jax.random.fold_in(stream_key, axis), (), 0, length) for axis, length in enumerate(result.shape)]
        where[longest] = (where[longest] + shift) % result.shape[longest]
        spots.append(tuple(where))
    return result.at[spots[0]].set(low).at[spots[1]].set(top_value)


def steps_of(rng, extent, cuts, least, top_value):
    loudness = 1.0
    for dim, shards_of in cuts:
        draws = jax.random.uniform(jax.random.fold_in(jax.random.fold_in(rng, 6), dim), (shards_of,), jnp.float32, least / len(cuts), top_value / len(cuts))
        loudness = loudness * jnp.repeat(jnp.exp(draws), extent[dim] // shards_of).reshape((-1,) + (1,) * (len(extent) - 1 - dim))
    return loudness


def centred(own_key, dims, scale, most, cuts=(), dtype=jnp.bfloat16):
    factor_of = steps_of(own_key, dims, cuts, -0.22, 0.18) if cuts else 1.0
    drawn = jax.random.normal(own_key, dims, jnp.float32) * scale * factor_of
    return jnp.minimum(jnp.maximum(drawn, -most), most).astype(dtype)


def setup_inputs(seed: int = 0) -> dict:
    splits = jax.random.split(jax.random.key(seed), 24)
    return {
        "tokens": centred(splits[0], (SEQS, SEQ, D), 1.0, 6.0, ((0, 32),)),
        "lengths": draw_lengths(jax.random.fold_in(splits[23], 71), 0),
        "query_lengths": plant(jax.random.randint(splits[2], (SEQS,), 2, SEQ // 8 + 1), jax.random.fold_in(splits[2], 1), 2, (SEQ // 8 + 1) - 1).astype(jnp.int32),
        "language_ids": plant(jax.random.randint(splits[3], (SEQS,), 0, NLANG), jax.random.fold_in(splits[3], 1), 0, NLANG - 1).astype(jnp.int32),
        "position_table": centred(splits[4], (SEQ, D), 0.5, 3.0, ((0, 8), (1, 4))),
        "segment_table": centred(splits[5], (2, D), 0.5, 3.0),
        "language_table": centred(splits[6], (NLANG, D), 0.5, 3.0),
        "query_weight": centred(splits[7], (D, D), D ** -0.5, 0.21875, ((0, 8), (1, 4))),
        "key_weight": centred(splits[8], (D, D), D ** -0.5, 0.21875, ((0, 8), (1, 4))),
        "value_weight": centred(splits[9], (D, D), D ** -0.5, 0.21875, ((0, 8), (1, 4))),
        "output_weight": centred(splits[10], (D, D), (D // 16) ** -0.5, 0.875, ((0, 8), (1, 4))),
        "query_bias": centred(splits[11], (D,), 0.3, 2.0),
        "value_bias": centred(splits[12], (D,), 0.3, 2.0),
        "output_bias": centred(splits[13], (D,), 0.3, 2.0),
        "first_gain": jnp.clip(1.0 + 0.1 * jax.random.normal(splits[14], (D,), jnp.float32), 0.5, 1.5).astype(jnp.bfloat16),
        "first_shift": centred(splits[15], (D,), 0.3, 2.0),
        "up_weight": centred(splits[16], (D, FF), D ** -0.5, 0.21875, ((0, 8), (1, 4))),
        "up_bias": centred(splits[17], (FF,), 0.3, 2.0),
        "down_weight": centred(splits[18], (FF, D), FF ** -0.5, 0.109375, ((0, 8), (1, 4))),
        "down_bias": centred(splits[19], (D,), 0.3, 2.0),
        "second_gain": jnp.clip(1.0 + 0.1 * jax.random.normal(splits[20], (D,), jnp.float32), 0.5, 1.5).astype(jnp.bfloat16),
        "second_shift": centred(splits[21], (D,), 0.3, 2.0),
        "cotangent": centred(splits[22], (SEQS, SEQ, D), 1.0, 6.0, ((0, 32),)),
    }


EPSILON = 1e-05
HIGHEST_PRECISION = lax.Precision.HIGHEST

@jax.custom_vjp
def low(v):
    return lax.optimization_barrier(v.astype(jnp.bfloat16)).astype(jnp.float32)

@jax.custom_vjp
def low_back(v):
    return v

def low_keep(v):
    return (low(v), None)

def low_pass(kept, grad):
    return (grad,)

def back_keep(v):
    return (v, None)

def back_low(kept, grad):
    return (low(grad),)
low.defvjp(low_keep, low_pass)
low_back.defvjp(back_keep, back_low)

def product(left_side, right_side):
    return jnp.dot(left_side, right_side, precision=HIGHEST_PRECISION)

def normalize(inputs, scales, offset):
    average = lax.optimization_barrier(jnp.mean(inputs, axis=-1, keepdims=True))
    centered = inputs - average
    spread = lax.optimization_barrier(jnp.mean(centered * centered, axis=-1, keepdims=True))
    return centered * lax.rsqrt(spread + EPSILON) * scales + offset

def attend(pieces):
    query_rows, key_rows, value_rows, length = pieces
    factor = 1.0 / math.sqrt(HD)
    scores = low_back(jnp.einsum('qhd,khd->hqk', query_rows, key_rows, precision=HIGHEST_PRECISION) * factor)
    keeping = jnp.arange(SEQ) < length
    scores = jnp.where(keeping[None, None, :], scores, -1e+30)
    row_max = lax.optimization_barrier(jnp.max(scores, axis=2, keepdims=True))
    weights = jnp.exp(scores - row_max)
    probabilities = weights / lax.optimization_barrier(jnp.sum(weights, axis=2, keepdims=True))
    return jnp.einsum('hqk,khd->qhd', low(probabilities), value_rows, precision=HIGHEST_PRECISION)

def forward(params, group_tokens, group_lengths, group_queries, group_languages):
    position_table, segment_table, language_table, query_weight, key_weight, value_weight, output_weight, query_bias, value_bias, output_bias, first_gain, first_shift, up_weight, up_bias, down_weight, down_bias, second_gain, second_shift = params
    group_size = group_tokens.shape[0]
    places = jnp.arange(SEQ)
    segment = (places[None, :] >= group_queries[:, None]).astype(jnp.int32)
    start = group_tokens + position_table[None] + segment_table[segment] + language_table[group_languages][:, None, :]
    flattened = start.reshape(group_size * SEQ, D)
    first_in = low(flattened)
    query_rows = low_back(low(product(first_in, query_weight) + query_bias))
    key_rows = low_back(low(product(first_in, key_weight)))
    value_rows = low_back(low(product(first_in, value_weight) + value_bias))
    split_shape = (group_size, SEQ, H, HD)
    context = lax.map(jax.checkpoint(attend), (query_rows.reshape(split_shape), key_rows.reshape(split_shape), value_rows.reshape(split_shape), group_lengths))
    context = low_back(low(context.reshape(group_size * SEQ, D)))
    attended = low_back(product(context, output_weight) + output_bias)
    first_out = normalize(flattened + attended, first_gain, first_shift)
    second_in = low(first_out)
    hidden_pre = low_back(product(second_in, up_weight) + up_bias)
    hidden = low(jax.nn.gelu(hidden_pre, approximate=False))
    branch = low_back(product(hidden, down_weight) + down_bias)
    final = normalize(first_out + branch, second_gain, second_shift)
    return final.reshape(group_size, SEQ, D)

def reference(tokens, lengths, query_lengths, language_ids, position_table, segment_table, language_table, query_weight, key_weight, value_weight, output_weight, query_bias, value_bias, output_bias, first_gain, first_shift, up_weight, up_bias, down_weight, down_bias, second_gain, second_shift, cotangent):
    params = tuple((item.astype(jnp.float32) for item in (position_table, segment_table, language_table, query_weight, key_weight, value_weight, output_weight, query_bias, value_bias, output_bias, first_gain, first_shift, up_weight, up_bias, down_weight, down_bias, second_gain, second_shift)))
    per_group = math.gcd(SEQS, max(1, 4096 // SEQ))
    groups = SEQS // per_group

    def shaped(array):
        return array.reshape((groups, per_group) + array.shape[1:])

    def one_group(summed, group_inputs):
        group_tokens, group_lengths, group_queries, group_languages, group_cotangent = group_inputs

        def run(params_in, tokens_in):
            return forward(params_in, tokens_in, group_lengths, group_queries, group_languages)
        group_out, puller = jax.vjp(run, params, group_tokens.astype(jnp.float32))
        param_grads, tokens_back = puller(group_cotangent.astype(jnp.float32))
        summed = jax.tree.map(jnp.add, summed, param_grads)
        return (summed, (group_out.astype(jnp.bfloat16), tokens_back.astype(jnp.bfloat16)))
    initial = tuple((jnp.zeros_like(item) for item in params))
    summed, (outputs, token_grads) = lax.scan(one_group, initial, (shaped(tokens), shaped(lengths), shaped(query_lengths), shaped(language_ids), shaped(cotangent)))
    return (outputs.reshape(SEQS, SEQ, D), token_grads.reshape(SEQS, SEQ, D), summed[0], summed[1], summed[2], summed[3], summed[4], summed[5], summed[6], summed[7], summed[8], summed[9], summed[10], summed[11], summed[12], summed[13], summed[14], summed[15], summed[16], summed[17])
```

```python
import math

import jax
import jax.numpy as jnp
from jax import lax
from jax.experimental import pallas as pl
from jax.experimental.pallas import tpu as pltpu
from jax.sharding import PartitionSpec as P

H = 12
HD = 64
EPSILON = 1e-05
NEG = -1e30


def normalize(inputs, scales, offset):
    average = jnp.mean(inputs, axis=-1, keepdims=True)
    centered = inputs - average
    spread = jnp.mean(centered * centered, axis=-1, keepdims=True)
    return centered * lax.rsqrt(spread + EPSILON) * scales + offset


def matmul(left_side, right_side):
    return jnp.dot(left_side, right_side, preferred_element_type=jnp.float32)


def matmul_first_t(left_side, right_side):
    return lax.dot_general(
        left_side, right_side, (((0,), (0,)), ((), ())), preferred_element_type=jnp.float32
    )


def matmul_second_t(left_side, right_side):
    return lax.dot_general(
        left_side, right_side, (((1,), (1,)), ((), ())), preferred_element_type=jnp.float32
    )


def exact_gelu(inputs):
    return jax.nn.gelu(inputs, approximate=False)


LANES = 384


def swap_partners(values, axis_name, mask):
    count = lax.axis_size(axis_name)
    return lax.ppermute(values, axis_name, [(i, i ^ mask) for i in range(count)])


def fold(shard):
    rows, cols = shard.shape
    if cols >= LANES:
        parts = cols // LANES
        return shard.reshape(rows, parts, LANES).transpose(1, 0, 2).reshape(rows * parts, LANES)
    parts = LANES // cols
    return shard.reshape(parts, rows // parts, cols).transpose(1, 0, 2).reshape(-1, LANES)


def unfold(folded, rows, cols):
    if cols >= LANES:
        parts = cols // LANES
        return folded.reshape(parts, rows, LANES).transpose(1, 0, 2).reshape(rows, cols)
    parts = LANES // cols
    return folded.reshape(-1, parts, cols).transpose(1, 0, 2).reshape(rows, cols)


def gather_pieces(folded):
    narrow_count = lax.axis_size("narrow")
    wide_count = lax.axis_size("wide")
    column = jnp.stack(
        [folded] + [swap_partners(folded, "narrow", k) for k in range(1, narrow_count)]
    )
    chips = [column] + [swap_partners(column, "wide", 2 * k) for k in range(1, wide_count // 2)]
    pieces = []
    for piece in chips:
        pieces += [piece, swap_partners(piece, "wide", 1)]
    return pieces


def scatter_sum(kept, sent):
    narrow_count = lax.axis_size("narrow")
    chip_count = lax.axis_size("wide") // 2
    wide32 = lambda values: values.astype(jnp.float32)
    arrived = swap_partners(sent, "wide", 1)
    sums = [
        (wide32(kept[k]) + wide32(arrived[k])).astype(jnp.bfloat16) for k in range(chip_count)
    ]
    total = wide32(sums[0])
    for k in range(1, chip_count):
        total = total + wide32(swap_partners(sums[k], "wide", 2 * k))
    total = total.astype(jnp.bfloat16)
    result = wide32(total[0])
    for k in range(1, narrow_count):
        result = result + wide32(swap_partners(total[k], "narrow", k))
    return result


def dot_nt(a,b): return lax.dot_general(a,b,(((1,),(1,)),((),())),preferred_element_type=jnp.float32)
def dot_nn(a,b): return lax.dot_general(a,b,(((1,),(0,)),((),())),preferred_element_type=jnp.float32)

def head_half(x, which):
    lane=lax.broadcasted_iota(jnp.int32,x.shape,1)
    keep=(lane<HD) if which==0 else (lane>=HD)
    return jnp.where(keep,x,jnp.zeros_like(x))

def mask_tail(s, live, length, fill):
    lo=s.shape[0]-128
    tail=s[lo:]
    key=lo+lax.broadcasted_iota(jnp.int32,tail.shape,0)
    tail=jnp.where(key<length,tail,fill)
    return tail if lo==0 else jnp.concatenate([s[:lo],tail],axis=0)

def fwd_kernel(len_ref,q_ref,k_ref,v_ref,o_ref,lse_ref):
    length=len_ref[pl.program_id(0)]
    nb=(length+127)//128
    seq=q_ref.shape[0]
    def run(live):
        k=k_ref[:live,:]
        vt=v_ref[:live,:].T
        q=q_ref[...]*jnp.bfloat16(0.125)
        outs=[];lses=[]
        for h in (0,1):
            s=dot_nt(k,head_half(q,h))
            s=mask_tail(s,live,length,NEG)
            m=jnp.max(s,axis=0,keepdims=True)
            p=jnp.exp(s-m)
            l=jnp.sum(p,axis=0,keepdims=True)
            low=(p*(1.0/l)).astype(jnp.bfloat16)
            outs.append(dot_nn(vt[h*HD:(h+1)*HD],low))
            lses.append(m+jnp.log(l))
        o_ref[...]=jnp.concatenate(outs,axis=0).T.astype(o_ref.dtype)
        lse_ref[...]=jnp.concatenate(lses,axis=0).reshape(lse_ref.shape)
    for j in range(1,seq//128+1):
        @pl.when(nb==j)
        def _(): run(j*128)

def bwd_kernel(len_ref,q_ref,k_ref,v_ref,do_ref,lse_ref,dq_ref,dk_ref,dv_ref):
    length=len_ref[pl.program_id(0)]
    nb=(length+127)//128
    seq=q_ref.shape[0]
    def run(live):
        k=k_ref[:live,:]
        v=v_ref[:live,:]
        kt=k.T
        q=q_ref[...]*jnp.bfloat16(0.125)
        do=do_ref[...]
        lse=lse_ref[...].reshape(2,seq)
        dk=None;dv=None;dqs=[]
        for h in (0,1):
            qh=head_half(q,h); doh=head_half(do,h)
            s=dot_nt(k,qh)
            s=mask_tail(s,live,length,NEG)
            p=jnp.exp(s-lse[h:h+1])
            dp=dot_nt(v,doh)
            delta=jnp.sum(p*dp,axis=0,keepdims=True)
            ds=(p*(dp-delta)).astype(jnp.bfloat16)
            low=p.astype(jnp.bfloat16)
            a=dot_nn(low,doh); b=dot_nn(ds,qh)
            dv=a if dv is None else dv+a
            dk=b if dk is None else dk+b
            dqs.append(dot_nn(kt[h*HD:(h+1)*HD],ds))
        dq_ref[...]=(jnp.concatenate(dqs,axis=0).T*0.125).astype(dq_ref.dtype)
        dk_ref[:live,:]=dk.astype(dk_ref.dtype)
        dv_ref[:live,:]=dv.astype(dv_ref.dtype)
        if live<seq:
            dk_ref[live:,:]=jnp.zeros((seq-live,128),dk_ref.dtype)
            dv_ref[live:,:]=jnp.zeros((seq-live,128),dv_ref.dtype)
    for j in range(1,seq//128+1):
        @pl.when(nb==j)
        def _(): run(j*128)

def attention_forward(lengths,q,k,v,pairs,seq):
    groups=q.shape[1]//128
    spec=pl.BlockSpec((seq,128),lambda b,g,n:(b,g))
    lspec=pl.BlockSpec((1,1,2,seq),lambda b,g,n:(b,g,0,0))
    return pl.pallas_call(fwd_kernel,
        grid_spec=pltpu.PrefetchScalarGridSpec(num_scalar_prefetch=1,grid=(pairs,groups),
            in_specs=[spec,spec,spec],out_specs=[spec,lspec]),
        out_shape=[jax.ShapeDtypeStruct(q.shape,jnp.bfloat16),jax.ShapeDtypeStruct((pairs,groups,2,seq),jnp.float32)],
        name='attention_forward',
    )(lengths,q,k,v)

def attention_backward(lengths,q,k,v,do,lse,pairs,seq):
    groups=q.shape[1]//128
    spec=pl.BlockSpec((seq,128),lambda b,g,n:(b,g))
    lspec=pl.BlockSpec((1,1,2,seq),lambda b,g,n:(b,g,0,0))
    return pl.pallas_call(bwd_kernel,
        grid_spec=pltpu.PrefetchScalarGridSpec(num_scalar_prefetch=1,grid=(pairs,groups),
            in_specs=[spec,spec,spec,spec,lspec],out_specs=[spec,spec,spec]),
        out_shape=[jax.ShapeDtypeStruct(q.shape,jnp.bfloat16)]*3,
        name='attention_backward',
    )(lengths,q,k,v,do,lse)


def on_device(
    tokens,
    lengths,
    query_lengths,
    language_ids,
    position_table,
    segment_table,
    language_table,
    query_weight,
    key_weight,
    value_weight,
    output_weight,
    query_bias,
    value_bias,
    output_bias,
    first_gain,
    first_shift,
    up_weight,
    up_bias,
    down_weight,
    down_bias,
    second_gain,
    second_shift,
    cotangent,
):
    seq_count, seq_len, features = tokens.shape
    row_count = seq_count * seq_len
    wide_count = lax.axis_size("wide")
    narrow_count = lax.axis_size("narrow")
    me_wide = lax.axis_index("wide")
    me_narrow = lax.axis_index("narrow")
    wide_order = lax.iota(jnp.int32, wide_count) ^ me_wide
    narrow_order = lax.iota(jnp.int32, narrow_count) ^ me_narrow

    def assembled(pieces, first_row, rows, cols):
        folded_rows = rows * cols // LANES
        stacked = jnp.stack([piece[:, first_row : first_row + folded_rows] for piece in pieces])
        stacked = jnp.take(jnp.take(stacked, wide_order, axis=0), narrow_order, axis=1)
        if cols >= LANES:
            blocks = stacked.reshape(wide_count, narrow_count, cols // LANES, rows, LANES)
            return blocks.transpose(0, 3, 1, 2, 4).reshape(wide_count * rows, narrow_count * cols)
        parts = LANES // cols
        blocks = stacked.reshape(wide_count, narrow_count, rows // parts, parts, cols)
        return blocks.transpose(0, 3, 2, 1, 4).reshape(wide_count * rows, narrow_count * cols)

    def assembled_down(pieces, first_row, rows, cols):
        folded_rows = rows * cols // LANES
        stacked = jnp.stack([piece[:, first_row : first_row + folded_rows] for piece in pieces])
        stacked = jnp.take(jnp.take(stacked, wide_order, axis=0), narrow_order, axis=1)
        if cols >= LANES:
            blocks = stacked.reshape(wide_count, narrow_count, cols // LANES, rows, LANES)
            return blocks.transpose(1, 3, 0, 2, 4).reshape(narrow_count * rows, wide_count * cols)
        parts = LANES // cols
        blocks = stacked.reshape(wide_count, narrow_count, rows // parts, parts, cols)
        return blocks.transpose(1, 3, 2, 0, 4).reshape(narrow_count * rows, wide_count * cols)

    def split_up(whole, rows, cols, transposed=False):
        whole = whole.astype(jnp.bfloat16)
        if cols >= LANES:
            if transposed:
                blocks = whole.reshape(narrow_count, rows, wide_count, cols // LANES, LANES)
                blocks = blocks.transpose(2, 0, 3, 1, 4)
            else:
                blocks = whole.reshape(wide_count, rows, narrow_count, cols // LANES, LANES)
                blocks = blocks.transpose(0, 2, 3, 1, 4)
        else:
            parts = LANES // cols
            if transposed:
                blocks = whole.reshape(narrow_count, parts, rows // parts, wide_count, cols)
                blocks = blocks.transpose(3, 0, 2, 1, 4)
            else:
                blocks = whole.reshape(wide_count, parts, rows // parts, narrow_count, cols)
                blocks = blocks.transpose(0, 3, 2, 1, 4)
        blocks = blocks.reshape(wide_count, narrow_count, rows * cols // LANES, LANES)
        return jnp.take(jnp.take(blocks, wide_order, axis=0), narrow_order, axis=1)

    def owner_sums(blocks):
        joined = jnp.concatenate(blocks, axis=2)
        chips = joined.reshape((wide_count // 2, 2) + joined.shape[1:])
        return scatter_sum(chips[:, 0], chips[:, 1])

    def shard_of(sums, first_row, rows, cols):
        return unfold(sums[first_row : first_row + rows * cols // LANES], rows, cols)

    position_rows, position_cols = position_table.shape
    weight_rows, weight_cols = query_weight.shape
    up_rows, up_cols = up_weight.shape
    down_rows, down_cols = down_weight.shape
    position_fold = position_rows * position_cols // LANES
    weight_fold = weight_rows * weight_cols // LANES
    up_fold = up_rows * up_cols // LANES
    down_fold = down_rows * down_cols // LANES

    first_pieces = gather_pieces(
        jnp.concatenate(
            [fold(position_table), fold(query_weight), fold(key_weight), fold(value_weight)]
        )
    )
    later_pieces = gather_pieces(
        jnp.concatenate([fold(up_weight), fold(down_weight.T), fold(output_weight)])
    )
    position_full = assembled(first_pieces, 0, position_rows, position_cols)
    query_full, key_full, value_full = [
        assembled(first_pieces, position_fold + i * weight_fold, weight_rows, weight_cols)
        for i in range(3)
    ]
    up_full = assembled(later_pieces, 0, up_rows, up_cols)
    down_across = assembled_down(later_pieces, up_fold, down_cols, down_rows)
    output_full = assembled(later_pieces, up_fold + down_fold, weight_rows, weight_cols)
    places = lax.broadcasted_iota(jnp.int32, (seq_count, seq_len), 1)
    passage = (places >= query_lengths[:, None])[:, :, None]
    segment_float = segment_table.astype(jnp.float32)
    segment_rows = jnp.where(passage, segment_float[1], segment_float[0])
    language_count = language_table.shape[0]
    language_hot = (
        language_ids[:, None] == lax.broadcasted_iota(jnp.int32, (seq_count, language_count), 1)
    ).astype(jnp.bfloat16)
    language_rows = matmul(language_hot, language_table)
    start = (
        tokens.astype(jnp.float32)
        + position_full.astype(jnp.float32)[None]
        + segment_rows
        + language_rows[:, None, :]
    )
    flattened = start.reshape(row_count, features)
    first_in = flattened.astype(jnp.bfloat16)
    query_rows = (matmul(first_in, query_full) + query_bias.astype(jnp.float32)).astype(
        jnp.bfloat16
    )
    key_rows = matmul(first_in, key_full).astype(jnp.bfloat16)
    value_rows = (matmul(first_in, value_full) + value_bias.astype(jnp.float32)).astype(
        jnp.bfloat16
    )
    context, log_totals = attention_forward(
        lengths, query_rows, key_rows, value_rows, seq_count, seq_len
    )
    attended = matmul(context, output_full) + output_bias.astype(jnp.float32)
    first_out, first_pull = jax.vjp(
        normalize,
        flattened + attended,
        first_gain.astype(jnp.float32),
        first_shift.astype(jnp.float32),
    )
    second_in = first_out.astype(jnp.bfloat16)
    hidden_pre = matmul(second_in, up_full) + up_bias.astype(jnp.float32)
    hidden = exact_gelu(hidden_pre).astype(jnp.bfloat16)
    branch = matmul_second_t(hidden, down_across) + down_bias.astype(jnp.float32)
    final, second_pull = jax.vjp(
        normalize,
        first_out + branch,
        second_gain.astype(jnp.float32),
        second_shift.astype(jnp.float32),
    )
    layer_out = final.astype(jnp.bfloat16).reshape(seq_count, seq_len, features)
    grad_second, second_gain_grad, second_shift_grad = second_pull(
        cotangent.astype(jnp.float32).reshape(row_count, features)
    )
    grad_branch = grad_second.astype(jnp.bfloat16)
    down_bias_grad = jnp.sum(grad_branch.astype(jnp.float32), axis=0)
    down_across_grad = matmul_first_t(grad_branch, hidden)
    gelu_value, gelu_pull = jax.vjp(exact_gelu, hidden_pre)
    grad_hidden = gelu_pull(matmul(grad_branch, down_across))[0].astype(jnp.bfloat16)
    up_bias_grad = jnp.sum(grad_hidden.astype(jnp.float32), axis=0)
    up_weight_grad = matmul_first_t(second_in, grad_hidden)
    forward_sums = owner_sums(
        [
            split_up(up_weight_grad, up_rows, up_cols),
            split_up(down_across_grad, down_cols, down_rows, True),
        ]
    )
    grad_first_out = grad_second + matmul_second_t(grad_hidden, up_full)
    grad_first, first_gain_grad, first_shift_grad = first_pull(grad_first_out)
    grad_attended = grad_first.astype(jnp.bfloat16)
    output_bias_grad = jnp.sum(grad_attended.astype(jnp.float32), axis=0)
    output_weight_grad = matmul_first_t(context, grad_attended)
    grad_context = matmul_second_t(grad_attended, output_full).astype(jnp.bfloat16)
    grad_query, grad_key, grad_value = attention_backward(
        lengths, query_rows, key_rows, value_rows, grad_context, log_totals, seq_count, seq_len
    )
    query_bias_grad = jnp.sum(grad_query.astype(jnp.float32), axis=0)
    value_bias_grad = jnp.sum(grad_value.astype(jnp.float32), axis=0)
    query_weight_grad = matmul_first_t(first_in, grad_query)
    key_weight_grad = matmul_first_t(first_in, grad_key)
    value_weight_grad = matmul_first_t(first_in, grad_value)
    grad_start = (
        grad_first
        + matmul_second_t(grad_query, query_full)
        + matmul_second_t(grad_key, key_full)
        + matmul_second_t(grad_value, value_full)
    )
    token_grad = grad_start.astype(jnp.bfloat16).reshape(seq_count, seq_len, features)
    grad_start_pairs = grad_start.reshape(seq_count, seq_len, features)
    position_local = jnp.sum(grad_start_pairs, axis=0)
    segment_local = jnp.stack(
        [
            jnp.sum(jnp.where(passage, 0.0, grad_start_pairs), axis=(0, 1)),
            jnp.sum(jnp.where(passage, grad_start_pairs, 0.0), axis=(0, 1)),
        ]
    )
    attention_sums = owner_sums(
        [split_up(position_local, position_rows, position_cols)]
        + [
            split_up(grad, weight_rows, weight_cols)
            for grad in (query_weight_grad, key_weight_grad, value_weight_grad, output_weight_grad)
        ]
    )
    small = jnp.concatenate(
        [
            jnp.sum(grad_start_pairs, axis=1),
            jnp.broadcast_to(language_ids.astype(jnp.float32)[:, None], (seq_count, features)),
            segment_local,
            query_bias_grad[None],
            value_bias_grad[None],
            output_bias_grad[None],
            first_gain_grad[None],
            first_shift_grad[None],
            down_bias_grad[None],
            second_gain_grad[None],
            second_shift_grad[None],
            up_bias_grad.reshape(-1, features),
        ]
    )
    everyone = jnp.stack(gather_pieces(small))
    everyone = jnp.take(jnp.take(everyone, wide_order, axis=0), narrow_order, axis=1)
    everyone = everyone.reshape((wide_count * narrow_count,) + small.shape)
    pair_sums = everyone[:, :seq_count].reshape(-1, features)
    pair_ids = everyone[:, seq_count : 2 * seq_count, 0].reshape(-1).astype(jnp.int32)
    small_sums = jnp.sum(everyone[:, 2 * seq_count :], axis=0)
    language_count_all = lax.broadcasted_iota(jnp.int32, (language_count, pair_ids.shape[0]), 0)
    language_sums = jnp.dot(
        (language_count_all == pair_ids[None]).astype(jnp.float32),
        pair_sums,
        precision=lax.Precision.HIGHEST,
    )
    weight_sums = [
        shard_of(attention_sums, position_fold + i * weight_fold, weight_rows, weight_cols)
        for i in range(4)
    ]
    return (
        layer_out,
        token_grad,
        shard_of(attention_sums, 0, position_rows, position_cols),
        small_sums[:2],
        language_sums,
        weight_sums[0],
        weight_sums[1],
        weight_sums[2],
        weight_sums[3],
        small_sums[2],
        small_sums[3],
        small_sums[4],
        small_sums[5],
        small_sums[6],
        shard_of(forward_sums, 0, up_rows, up_cols),
        small_sums[10:].reshape(-1),
        shard_of(forward_sums, up_fold, down_cols, down_rows).T,
        small_sums[7],
        small_sums[8],
        small_sums[9],
    )


def solution(mesh):
    return jax.shard_map(
        on_device,
        mesh=mesh,
        in_specs=(
            P(("wide", "narrow"), None, None),
            P(("wide", "narrow")),
            P(("wide", "narrow")),
            P(("wide", "narrow")),
            P("wide", "narrow"),
            P(),
            P(),
            P("wide", "narrow"),
            P("wide", "narrow"),
            P("wide", "narrow"),
            P("wide", "narrow"),
            P(),
            P(),
            P(),
            P(),
            P(),
            P("wide", "narrow"),
            P(),
            P("wide", "narrow"),
            P(),
            P(),
            P(),
            P(("wide", "narrow"), None, None),
        ),
        out_specs=(
            P(("wide", "narrow"), None, None),
            P(("wide", "narrow"), None, None),
            P("wide", "narrow"),
            P(),
            P(),
            P("wide", "narrow"),
            P("wide", "narrow"),
            P("wide", "narrow"),
            P("wide", "narrow"),
            P(),
            P(),
            P(),
            P(),
            P(),
            P("wide", "narrow"),
            P(),
            P("wide", "narrow"),
            P(),
            P(),
            P(),
        ),
        check_vma=False,
    )
```
